128 devices in a mesh: occ: 4 (over x), vir: 32 (over y, z, core).
Axes of the slice: x: 4, y: 4, z: 4, core: 2. Of those that a mesh axis runs over, the one named last changes fastest.
Arguments:
- amplitudes: bfloat16 [256, 262144], P('occ', 'vir'), may hold values from -6 to 6
- cycle_integrals: bfloat16 [16, 64, 16, 64], P(None, None, 'occ'), may hold values from -0.1875 to 0.1875
- ladder_tiles: bfloat16 [2048, 4, 128, 128], P('vir'), may hold values from -0.25 to 0.25
- ladder_rows: int32 [2048, 4], P('vir'), may hold values from 0 to 2047, as said below
- ladder_count: int32 [2048], P('vir'), may hold values from 2 to 4
- row_gap: float32 [256], P('occ'), may hold values from 1 to 3
- column_energy: float32 [262144], P('vir'), may hold values from 0.5 to 8
Outputs:
- updated: bfloat16 [256, 262144], P('occ', 'vir')
The draws below stay inside these ranges and needn't reach their ends.
Inputs may be any that keep to these rules, and one draw needn't show every extreme that they name: `ladder_rows`: each entry of column tile c's list names a virtual-pair tile within 2 tiles of c; entry 0 is max(c - 2, 0) and entry 1 is min(c + 2, 2047).
All inputs are finite; a program needn't handle non-finite values.
Results may differ from the reference program's by a relative error of at most 0.0019.
Values may be sent and summed in bfloat16 or wider, within the bound.
A program may use at most 192 MiB of HBM per device.

```python
import math
import jax
import jax.numpy as jnp
from jax import lax

TILE = 128
NJ = 16
NA = 4096
KMAX = 4
HT = 2
NI = 16
NB = 64
ROWS = 256
COLS = 262144
CTT = 2048


def draw_ladder_rows(key, part):
    shifts = jax.random.randint(key, (CTT, KMAX), -HT, HT + 1).astype(jnp.int32)
    entry = jnp.arange(KMAX, dtype=jnp.int32)[None, :]
    shifts = jnp.where(entry == 0, -HT, jnp.where(entry == 1, HT, shifts)).astype(jnp.int32)
    column_tiles = jnp.arange(CTT, dtype=jnp.int32)[:, None]
    return jnp.clip(column_tiles + shifts, 0, CTT - 1).astype(jnp.int32)


def set_ends(array, rng, smallest, high):
    place = [jax.random.randint(jax.random.fold_in(rng, axis), (), 0, length) for axis, length in enumerate(array.shape)]
    longest = array.shape.index(max(array.shape))
    next_to = place[:longest] + [(place[longest] + 1) % array.shape[longest]] + place[longest + 1:]
    return array.at[tuple(place)].set(smallest).at[tuple(next_to)].set(high)


def levels(key, shape, shards, least, top_value):
    def one(position, blocks):
        heights = jax.random.uniform(jax.random.fold_in(jax.random.fold_in(key, 6), position), (blocks,), jnp.float32, least / len(shards), top_value / len(shards))
        return jnp.repeat(jnp.exp(heights), shape[position] // blocks).reshape((-1,) + (1,) * (len(shape) - position - 1))

    level = one(*shards[0])
    for cut in shards[1:]:
        level = level * one(*cut)
    return level


def scatter_about(stream_key, shape, spread, limit, split=(), held_as=jnp.bfloat16):
    loudness = levels(stream_key, shape, split, -0.22, 0.18) if split else 1.0
    values = jax.random.normal(stream_key, shape, jnp.float32) * spread * loudness
    return jnp.minimum(jnp.maximum(values, -limit), limit).astype(held_as)


def setup_inputs(seed: int = 0) -> dict:
    keys = jax.random.split(jax.random.key(seed), 8)
    amplitudes = scatter_about(keys[0], (ROWS, COLS), 1.0, 6.0, ((0, 4), (1, 32)))
    cycle_integrals = scatter_about(keys[1], (NJ, NB, NJ, NB), (NJ * NB) ** -0.5, 0.1875, ((2, 4),))
    ladder_tiles = scatter_about(keys[2], (CTT, KMAX, TILE, TILE), (KMAX * TILE) ** -0.5, 0.25, ((0, 32),))
    ladder_rows = draw_ladder_rows(jax.random.fold_in(keys[7], 71), 0)
    ladder_count = set_ends(jax.random.randint(keys[4], (CTT,), 2, KMAX + 1), jax.random.fold_in(keys[4], 1), 2, KMAX).astype(jnp.int32)
    row_gap = jnp.clip(1.0 + 2.0 * jax.random.uniform(keys[5], (ROWS,), jnp.float32) ** levels(keys[5], (ROWS,), ((0, 4),), -0.2, 0.2), 1.0, 3.0)
    column_energy = jnp.clip(jnp.exp(math.log(8.0) - 2.7725887 * jax.random.uniform(keys[6], (COLS,), jnp.float32) ** levels(keys[6], (COLS,), ((0, 32),), -0.2, 0.2)), 0.5, 8.0)
    return {"amplitudes": amplitudes, "cycle_integrals": cycle_integrals, "ladder_tiles": ladder_tiles, "ladder_rows": ladder_rows, "ladder_count": ladder_count, "row_gap": row_gap, "column_energy": column_energy}


def reference(amplitudes, cycle_integrals, ladder_tiles, ladder_rows, ladder_count, row_gap, column_energy):
    cycle_float = cycle_integrals.astype(jnp.float32)
    blocks = amplitudes.reshape(NI, NJ, NB, NA)

    def cycle_block(amp_block):
        return jnp.einsum('jba,jbkc->kca', amp_block.astype(jnp.float32), cycle_float).astype(jnp.bfloat16)

    cycle = lax.map(cycle_block, blocks).reshape(ROWS, COLS)
    tiled = amplitudes.reshape(ROWS, CTT, TILE)

    def tile_update(inputs):
        tile_index, rows_list, count_one, tiles_one = inputs
        picked = jnp.take(tiled, rows_list, axis=1)
        live_mask = jnp.arange(KMAX, dtype=jnp.int32) < count_one
        live_tiles = jnp.where(live_mask[:, None, None], tiles_one, jnp.zeros((), jnp.bfloat16))
        ladder = jnp.einsum('rkp,kpq->rq', picked.astype(jnp.float32), live_tiles.astype(jnp.float32))
        offset = (tile_index * TILE).astype(jnp.int32)
        cycle_part = lax.dynamic_slice_in_dim(cycle, offset, TILE, 1)
        old_part = lax.dynamic_slice_in_dim(amplitudes, offset, TILE, 1)
        energy = lax.dynamic_slice_in_dim(column_energy, offset, TILE, 0)
        denominator = row_gap[:, None] + energy[None, :]
        return (old_part.astype(jnp.float32) + (cycle_part.astype(jnp.float32) + ladder) / denominator).astype(jnp.bfloat16)

    result = lax.map(tile_update, (jnp.arange(CTT, dtype=jnp.int32), ladder_rows, ladder_count, ladder_tiles))
    return jnp.transpose(result, (1, 0, 2)).reshape(ROWS, COLS)
```

```python
import jax
import jax.numpy as jnp
from jax import lax
from jax.experimental import pallas as pl
from jax.experimental.pallas import tpu as pltpu
from jax.sharding import PartitionSpec as P

TILE = 128
NV = 32
NO = 4
TILES = 64
MESH = pl.DeviceIdType.MESH
F32 = jnp.float32
BF16 = jnp.bfloat16


def lanes(tile):
    return pl.ds(pl.multiple_of(tile * TILE, TILE), TILE)


def kernel(
    rows_ref, count_ref, amp_ref, w_ref, tiles_ref, gap_ref, energy_ref, out_ref,
    near, tiles, spread, spread_wide, w_all, w_rows, back, landed, base, inverse,
    near_sem, tiles_sem, own_sem, w_own_sem, back_own_sem,
    halo_send, halo_recv, spread_send, spread_recv,
    w_send, w_recv, pass_send, pass_recv, back_send, back_recv,
):
    x = lax.axis_index("occ")
    v = lax.axis_index("vir")
    core = v % 2
    twin = v + 1 - 2 * core

    def load_tile(t):
        return pltpu.make_async_copy(amp_ref.at[:, lanes(t)], near.at[t + 2], near_sem.at[t])

    def load_ladder(q):
        return pltpu.make_async_copy(
            tiles_ref.at[pl.ds(q * 16, 16)], tiles.at[pl.ds(q * 16, 16)], tiles_sem.at[q]
        )

    def own_block(part):
        return pltpu.make_async_copy(
            amp_ref.at[:, lanes(part * NV + v)], spread.at[2 * v + part], own_sem.at[part]
        )

    own_w = pltpu.make_async_copy(w_ref, w_all.at[x], w_own_sem)

    @pl.loop(0, TILES)
    def _(t):
        load_tile(t).start()

    for q in range(4):
        load_ladder(q).start()
    own_w.start()
    for part in range(2):
        own_block(part).start()

    barrier = pltpu.get_barrier_semaphore()

    @pl.loop(1, NV)
    def _(d):
        pl.semaphore_signal(barrier, inc=1, device_id=(x, (v + d) % NV), device_id_type=MESH)

    for d in range(1, NO):
        pl.semaphore_signal(barrier, inc=1, device_id=((x + d) % NO, v), device_id_type=MESH)
    pl.semaphore_wait(barrier, NV - 1 + NO - 1)

    def halo(index):
        side, part = index // 2, index % 2
        tile = TILES - 2 + part if side == 0 else part
        slot = part if side == 0 else TILES + 2 + part
        peer = (v + 1) % NV if side == 0 else (v + NV - 1) % NV
        return pltpu.make_async_remote_copy(
            src_ref=amp_ref.at[:, tile * TILE : (tile + 1) * TILE],
            dst_ref=near.at[slot],
            send_sem=halo_send.at[index],
            recv_sem=halo_recv.at[index],
            device_id=(x, peer),
            device_id_type=MESH,
        )

    half = pl.ds(pl.multiple_of(core * 128, 128), 128)
    other_half = pl.ds(pl.multiple_of(128 - core * 128, 128), 128)

    def w_out(d, owner):
        return pltpu.make_async_remote_copy(
            src_ref=w_ref.at[half],
            dst_ref=w_all.at[owner, half],
            send_sem=w_send.at[d],
            recv_sem=w_recv.at[d],
            device_id=((x + d) % NO, v),
            device_id_type=MESH,
        )

    def w_pass(d, rows):
        owner = (x + NO - d) % NO
        return pltpu.make_async_remote_copy(
            src_ref=w_all.at[owner, rows],
            dst_ref=w_all.at[owner, rows],
            send_sem=pass_send.at[d],
            recv_sem=pass_recv.at[d],
            device_id=(x, twin),
            device_id_type=MESH,
        )

    def spread_out(d, part, source):
        target = (v + d) % NV
        return pltpu.make_async_remote_copy(
            src_ref=amp_ref.at[:, lanes(part * NV + target)],
            dst_ref=spread.at[2 * source + part],
            send_sem=spread_send.at[d, part],
            recv_sem=spread_recv.at[d, part],
            device_id=(x, target),
            device_id_type=MESH,
        )

    for index in range(4):
        halo(index).start()
    for d in (2, 1, 3):
        w_out(d, x).start()

    @pl.loop(1, NV)
    def _(d):
        for part in range(2):
            spread_out(d, part, v).start()

    near[TILES + 4] = jnp.zeros((64, TILE), BF16)
    row = lax.broadcasted_iota(jnp.int32, (64, 64), 0)
    column = lax.broadcasted_iota(jnp.int32, (64, 64), 1)
    gap = jnp.sum(jnp.where(row == column, gap_ref[...], 0.0), axis=1, keepdims=True)

    @pl.loop(0, TILES)
    def _(t):
        load_tile(t).wait()

    for index in range(4):
        halo(index).wait_recv()

    def ladder_tile(c):
        count = count_ref[c]
        picked = []
        for k in range(4):
            place = jnp.clip(rows_ref[k, c] - v * TILES + 2, 0, TILES + 3)
            if k >= 2:
                place = jnp.where(k < count, place, TILES + 4)
            picked.append(near[place])
        term = jnp.dot(jnp.concatenate(picked, axis=1), tiles[c], preferred_element_type=F32)
        scale = 1.0 / (gap + energy_ref[pl.ds(c, 1), :])
        inverse[c] = scale
        base[c] = near[c + 2].astype(F32) + term * scale

    for q in range(4):
        load_ladder(q).wait()

        @pl.loop(0, 4)
        def _(t):
            for step in range(4):
                ladder_tile(q * 16 + t * 4 + step)

    own_w.wait()
    for d in (1, 3, 2):
        w_out(d, (x + NO - d) % NO).wait_recv()
        w_pass(d, half).start()
    for d in (1, 3, 2):
        w_pass(d, other_half).wait_recv()

    r = lax.broadcasted_iota(jnp.int32, (256, 256), 0)
    c = lax.broadcasted_iota(jnp.int32, (256, 256), 1)
    source = ((r // 4) % 4) * 64 + (r // 16) * 4 + r % 4
    order = jnp.where(c == source, 1.0, 0.0).astype(BF16)
    for q in range(4):
        piece = jnp.concatenate([w_all[g, q * 64 : (q + 1) * 64, :] for g in range(NO)], axis=0)
        w_rows[q] = jnp.dot(order, piece, preferred_element_type=F32).astype(BF16)

    for part in range(2):
        own_block(part).wait()

    @pl.loop(1, NV)
    def _(d):
        for part in range(2):
            spread_out(d, part, (v + NV - d) % NV).wait_recv()

    for i in range(NO):
        spread_wide[:, i * TILE : (i + 1) * TILE] = spread[:, i * 16 : (i + 1) * 16, :].reshape(
            1024, TILE
        )

    group, member = v // 8, v % 8

    def back_out(s, e, origin):
        target = ((group + s) % 4) * 8 + (member + e) % 8
        return pltpu.make_async_remote_copy(
            src_ref=back.at[target],
            dst_ref=landed.at[origin],
            send_sem=back_send.at[s * 8 + e],
            recv_sem=back_recv.at[s * 8 + e],
            device_id=(x, target),
            device_id_type=MESH,
        )

    own_back = pltpu.make_async_copy(back.at[v], landed.at[v], back_own_sem)

    for s in range(4):
        q = (group + s) % 4
        product = jnp.dot(w_rows[q], spread_wide[...], preferred_element_type=F32).astype(BF16)
        for i in range(NO):
            back[pl.ds(q * 8, 8), :, i * 16 : (i + 1) * 16, :] = product[
                :, i * TILE : (i + 1) * TILE
            ].reshape(8, 2, 16, TILE)
        if s == 0:
            own_back.start()

        @pl.loop(1 if s == 0 else 0, 8)
        def _(e):
            back_out(s, e, v).start()

    def combine(origin):
        for part in range(2):
            tile = part * NV + origin
            value = base[tile] + landed[origin, part].astype(F32) * inverse[tile]
            out_ref[:, lanes(tile)] = value.astype(BF16)

    own_back.wait()
    combine(v)
    for s in range(4):

        @pl.loop(1 if s == 0 else 0, 8)
        def _(e):
            origin = ((group + 4 - s) % 4) * 8 + (member + 8 - e) % 8
            back_out(s, e, origin).wait_recv()
            combine(origin)

    for index in range(4):
        halo(index).wait_send()
    for d in range(1, NO):
        w_out(d, x).wait_send()
        w_pass(d, half).wait_send()

    @pl.loop(1, NV)
    def _(d):
        for part in range(2):
            spread_out(d, part, v).wait_send()

    for s in range(4):

        @pl.loop(1 if s == 0 else 0, 8)
        def _(e):
            back_out(s, e, v).wait_send()


def local(
    amplitudes, cycle_integrals, ladder_tiles, ladder_rows, ladder_count, row_gap, column_energy
):
    w_shard = jnp.transpose(cycle_integrals, (3, 2, 1, 0)).reshape(256, 1024)
    dma = pltpu.SemaphoreType.DMA
    any_space = pl.BlockSpec(memory_space=pl.ANY)
    smem = pl.BlockSpec(memory_space=pltpu.SMEM)
    vmem = pl.BlockSpec(memory_space=pltpu.VMEM)
    return pl.pallas_call(
        kernel,
        out_shape=jax.ShapeDtypeStruct((64, 8192), BF16),
        in_specs=[smem, smem, any_space, any_space, any_space, vmem, vmem],
        out_specs=vmem,
        scratch_shapes=[
            pltpu.VMEM((TILES + 5, 64, TILE), BF16),
            pltpu.VMEM((TILES, 512, TILE), BF16),
            pltpu.VMEM((64, 64, TILE), BF16),
            pltpu.VMEM((1024, 512), BF16),
            pltpu.VMEM((NO, 256, 1024), BF16),
            pltpu.VMEM((4, 256, 1024), BF16),
            pltpu.VMEM((NV, 2, 64, TILE), BF16),
            pltpu.VMEM((NV, 2, 64, TILE), BF16),
            pltpu.VMEM((TILES, 64, TILE), F32),
            pltpu.VMEM((TILES, 64, TILE), F32),
            dma((TILES,)),
            dma((4,)),
            dma((2,)),
            dma,
            dma,
            dma((4,)),
            dma((4,)),
            dma((NV, 2)),
            dma((NV, 2)),
            dma((NO,)),
            dma((NO,)),
            dma((NO,)),
            dma((NO,)),
            dma((NV,)),
            dma((NV,)),
        ],
        compiler_params=pltpu.CompilerParams(
            collective_id=0, has_side_effects=True, vmem_limit_bytes=60 * 2**20
        ),
    )(
        ladder_rows.T,
        ladder_count,
        amplitudes,
        w_shard,
        ladder_tiles.reshape(TILES, 512, TILE),
        row_gap.reshape(1, 64),
        column_energy.reshape(TILES, TILE),
    )


def solution(mesh):
    in_specs = (
        P("occ", "vir"),
        P(None, None, "occ", None),
        P("vir", None, None, None),
        P("vir", None),
        P("vir"),
        P("occ"),
        P("vir"),
    )
    return jax.shard_map(
        local, mesh=mesh, in_specs=in_specs, out_specs=P("occ", "vir"), check_vma=False
    )
```
